32 devices in a mesh: groups: 2 (over x), seq: 16 (over z, y, core).
Axes of the slice: x: 2, y: 2, z: 4, core: 2. Of those that a mesh axis runs over, the one named last changes fastest.
Arguments:
- tokens: bfloat16 [8192, 2048], P(('groups', 'seq')), parts along dimension 0, may hold values from -60 to 60
- w_query: bfloat16 [2048, 1024], P('seq'), may hold values from -0.125 to 0.125
- w_keyval: bfloat16 [2048, 2048], P('seq'), may hold values from -0.125 to 0.125
- global_off: int32 [32], P(('groups', 'seq')), parts along dimension 0, may hold values from 0 to 255
- rand_dev: int32 [128, 8, 3], P('groups'), parts along dimension 0, may hold values from 0 to 15, all different within a row; in each aligned block of 32 rows (0 to 31, 32 to 63, ..., all dimensions but the last counted through in order) at most 9 rows name the same one
- rand_sub: int32 [128, 8, 3], P('groups'), parts along dimension 0, may hold values from 0 to 3
Outputs:
- context: bfloat16 [8192, 1024], P(('groups', 'seq')), parts along dimension 0
The draws below stay inside these ranges and needn't reach their ends.
There are 2 independent parts, one for each index of `groups`. The reference program is written for one: setup_inputs(seed, part) draws one part's arguments, and reference() takes and returns one part's arrays. A program takes and returns all parts, laid end to end along the dimension named above; an argument that names none is the same for every part. Nothing has to cross between parts.
Inputs may be any that keep to these rules, and one draw needn't show every extreme that they name: Over the 4 query blocks of one shard and all heads, no shard is named by more than 9 entries of rand_dev, and this bound is reached in every draw; the 3 entries of one query block and head name different shards.
All inputs are finite; a program needn't handle non-finite values.
Results may differ from the reference program's by a relative error of at most 0.0045.
The reference program's roundings to bfloat16 on the way (of `query`, `keyval` and `weights`) count: a program that leaves them out, or rounds other values in their place, can miss the bound.
Values may be sent and summed in bfloat16 or wider, within the bound.
No kernel may reach another device: no remote copies, remote signals or barrier semaphores. Data moves between devices by JAX's collectives and lax.ppermute only.
A program may use at most 128 MiB of HBM per device.

```python
import math
import jax
import jax.numpy as jnp
import numpy as np
from jax import lax

D = 2048
H = 8
HD = 128
BLOCK = 64
R = 3
GLOB_DEV = 1
BLK_DEV = 4
TOK_DEV = 256
NB = 64
TOKENS = 4096
G = 16
CAP = 9
N_SEQ = 16


def draw_tokens(key, part):
    base = jnp.clip(jax.random.normal(key, (TOKENS, D), jnp.float32), -6.0, 6.0)
    return base.astype(jnp.bfloat16)


def touch_ends(entries, stream_key, low, top_value):
    longest = entries.shape.index(max(entries.shape))
    spots = []
    for shift in (0, 1):
        where = [jax.random.randint(jax.random.fold_in(stream_key, axis), (), 0, length) for axis, length in enumerate(entries.shape)]
        where[longest] = (where[longest] + shift) % entries.shape[longest]
        spots.append(tuple(where))
    return entries.at[spots[0]].set(low).at[spots[1]].set(top_value)


def block_scale(key, dims, cuts, smallest, largest):
    level = 1.0
    for axis_at, shards_of in cuts:
        steps = jax.random.uniform(jax.random.fold_in(jax.random.fold_in(key, 6), axis_at), (shards_of,), jnp.float32, smallest / len(cuts), largest / len(cuts))
        level = level * jnp.repeat(jnp.exp(steps), dims[axis_at] // shards_of).reshape((-1,) + (1,) * (len(dims) - 1 - axis_at))
    return level


def shared_out(rng, own, number, rows, count, top, reach, slope):
    ranking = jax.random.permutation(rng, count)
    packed, ordinary = portions_of(count, rows * top, reach, slope, True), portions_of(count, rows * top, reach, slope, False)
    places = jnp.arange(count)

    def named(tallies, rotation):
        used = int((tallies > 0).sum())
        fixed = max(1, used // 4)
        shifted = fixed + (places - fixed + rotation * (used - fixed)) % max(1, count - fixed)
        return jnp.zeros((count,), jnp.int32).at[ranking[jnp.where(places < fixed, places, shifted)]].set(jnp.asarray(tallies, jnp.int32))

    tallies = jnp.where(number % 4 == 0, named(packed, number // 4), named(ordinary, number - number // 4 - 1))
    mixed = jax.random.permutation(jax.random.fold_in(own, 3), count)
    donor, receiver = mixed[0:count // 2 * 2:2], mixed[1:count // 2 * 2:2]
    margin = jnp.minimum(tallies[donor] - 1, reach - tallies[receiver]) // 2
    margin = jnp.where((donor == ranking[0]) | (receiver == ranking[0]) | (tallies[receiver] == 0), 0, jnp.maximum(margin, 0))
    shifted = jax.random.randint(jax.random.fold_in(own, 4), (count // 2,), 0, 1 << 20) % (margin + 1)
    tallies = tallies.at[donor].add(-shifted).at[receiver].add(shifted)
    items = jnp.searchsorted(jnp.cumsum(tallies), jnp.arange(rows * top), side="right").astype(jnp.int32)
    table = items.reshape(top, rows).T
    table = table[jax.random.permutation(jax.random.fold_in(own, 1), rows)]
    rotation = jax.random.randint(jax.random.fold_in(own, 2), (rows, 1), 0, top)
    return jnp.take_along_axis(table, (jnp.arange(top)[None, :] + rotation) % top, axis=1)


def portions_of(number_of, total, limit, slope, full):
    weights = [(1 << 20) // math.isqrt(grade ** slope) + 1 for grade in range(1, number_of + 1)]
    largest = limit if full else min(limit, max(-(-total // number_of), total * weights[0] // sum(weights)))
    least = 1 if total - largest >= number_of - 1 else 0
    counts, spare = [largest] + [least] * (number_of - 1), total - largest - least * (number_of - 1)
    while spare > 0:
        free = [i for i in range(1, number_of) if counts[i] < largest] or [i for i in range(1, number_of) if counts[i] < limit]
        mass, remaining = sum([weights[i] for i in free]), spare
        for i in free:
            more = min(limit - counts[i], max(1, remaining * weights[i] // mass), spare)
            counts[i] = counts[i] + more
            spare = spare - more
    return np.array(counts)


def gaussian(rng, extent, scale, reach, shards=(), held_as=jnp.bfloat16):
    array = scale * jax.random.normal(rng, extent, jnp.float32)
    if shards:
        array = array * block_scale(rng, extent, shards, -0.22, 0.18)
    return jnp.clip(array, -reach, reach).astype(held_as)


def setup_inputs(seed: int = 0, part: int = 0) -> dict:
    seeds = jax.random.split(jax.random.key(seed), 7)
    own_keys = jax.random.split(jax.random.fold_in(seeds[6], part), 7)
    tokens = draw_tokens(jax.random.fold_in(jax.random.fold_in(seeds[6], part), 71), part)
    w_query = gaussian(seeds[1], (D, H * HD), D ** -0.5, 0.125, ((0, 16),))
    w_keyval = gaussian(seeds[2], (D, 2 * H * HD), D ** -0.5, 0.125, ((0, 16),))
    global_off = touch_ends(jax.random.randint(own_keys[3], (G,), 0, TOK_DEV), jax.random.fold_in(own_keys[3], 1), 0, TOK_DEV - 1).astype(jnp.int32)
    rand_dev_keys = jax.random.split(jax.random.fold_in(own_keys[4], 1), NB * H // (BLK_DEV * H))
    rand_dev_turns = jax.random.permutation(jax.random.fold_in(own_keys[4], 3), NB * H // (BLK_DEV * H))
    rand_dev = jax.vmap(lambda own, number: shared_out(jax.random.fold_in(own_keys[4], 2), own, number, BLK_DEV * H, N_SEQ, R, CAP, 1))(rand_dev_keys, rand_dev_turns).reshape((NB, H, R))
    rand_sub = touch_ends(jax.random.randint(own_keys[5], (NB, H, R), 0, BLK_DEV), jax.random.fold_in(own_keys[5], 1), 0, BLK_DEV - 1).astype(jnp.int32)
    return dict(tokens=tokens, w_query=w_query, w_keyval=w_keyval, global_off=global_off, rand_dev=rand_dev, rand_sub=rand_sub)


def reference(tokens, w_query, w_keyval, global_off, rand_dev, rand_sub):
    def project(rows):
        query = jnp.dot(rows, w_query, preferred_element_type=jnp.float32).astype(jnp.bfloat16)
        keyval = jnp.dot(rows, w_keyval, preferred_element_type=jnp.float32).astype(jnp.bfloat16)
        return query, keyval

    query, keyval = lax.map(project, tokens.reshape(N_SEQ, TOK_DEV, D))
    query = query.reshape(NB, BLOCK, H, HD)
    keyval = keyval.reshape(NB, BLOCK, 2, H, HD)
    positions = (jnp.arange(G, dtype=jnp.int32) // GLOB_DEV) * TOK_DEV + global_off
    glob = keyval.reshape(TOKENS, 2, H, HD)[positions].astype(jnp.float32)
    block_ids = rand_dev * BLK_DEV + rand_sub
    zero_blk = jnp.zeros((1, BLOCK, 2, H, HD), keyval.dtype)
    padded = jnp.concatenate([zero_blk, keyval, zero_blk], axis=0)
    head_ids = jnp.arange(H, dtype=jnp.int32)[None, :, None]
    scale = HD ** -0.5

    def attend(index):
        start = (index * BLK_DEV).astype(jnp.int32)
        qry = lax.dynamic_slice_in_dim(query, start, BLK_DEV, 0).astype(jnp.float32)
        win = jnp.concatenate([lax.dynamic_slice_in_dim(padded, start + j, BLK_DEV, 0) for j in range(3)], axis=1).astype(jnp.float32)
        ids = lax.dynamic_slice_in_dim(block_ids, start, BLK_DEV, 0)
        fetched = keyval[ids, :, :, head_ids, :].astype(jnp.float32)
        s_win = jnp.einsum('bqhd,bkhd->bhqk', qry, win[:, :, 0]) * scale
        s_rnd = jnp.einsum('bqhd,bhrkd->bhqrk', qry, fetched[:, :, :, :, 0]).reshape(BLK_DEV, H, BLOCK, R * BLOCK) * scale
        s_glb = jnp.einsum('bqhd,ghd->bhqg', qry, glob[:, 0]) * scale
        blk = start + jnp.arange(BLK_DEV, dtype=jnp.int32)
        left_ok = jnp.repeat((blk > 0)[:, None], BLOCK, axis=1)
        right_ok = jnp.repeat((blk < NB - 1)[:, None], BLOCK, axis=1)
        mid_ok = jnp.ones((BLK_DEV, BLOCK), dtype=bool)
        win_ok = jnp.concatenate([left_ok, mid_ok, right_ok], axis=1)
        s_win = jnp.where(win_ok[:, None, None, :], s_win, -jnp.inf)
        scores = jnp.concatenate([s_win, s_rnd, s_glb], axis=3)
        top = jnp.max(scores, axis=3, keepdims=True)
        expo = jnp.exp(scores - top)
        weights = (expo / jnp.sum(expo, axis=3, keepdims=True)).astype(jnp.bfloat16).astype(jnp.float32)
        w_win = weights[..., :3 * BLOCK]
        w_rnd = weights[..., 3 * BLOCK:3 * BLOCK + R * BLOCK].reshape(BLK_DEV, H, BLOCK, R, BLOCK)
        w_glb = weights[..., 3 * BLOCK + R * BLOCK:]
        ctx = jnp.einsum('bhqk,bkhd->bqhd', w_win, win[:, :, 1])
        ctx = ctx + jnp.einsum('bhqrk,bhrkd->bqhd', w_rnd, fetched[:, :, :, :, 1])
        ctx = ctx + jnp.einsum('bhqg,ghd->bqhd', w_glb, glob[:, 1])
        return ctx.astype(jnp.bfloat16)

    context = lax.map(attend, jnp.arange(N_SEQ, dtype=jnp.int32))
    return context.reshape(TOKENS, H * HD)
```

```python
import functools

import jax
import jax.numpy as jnp
from jax import lax
from jax.experimental import pallas as pl
from jax.experimental.pallas import tpu as pltpu
from jax.sharding import PartitionSpec as P

AXES = ("groups", "seq")


def shift_perm(nz, dg=0, dz=0, dy=0, dc=0):
    pairs = []
    for g in range(2):
        for z in range(nz):
            for y in range(2):
                for c in range(2):
                    here = ((g * nz + z) * 2 + y) * 2 + c
                    there = (((g ^ dg) * nz + (z + dz) % nz) * 2 + (y ^ dy)) * 2 + (c ^ dc)
                    pairs.append((here, there))
    return pairs


def send(nz, value, **step):
    return lax.ppermute(value, AXES, shift_perm(nz, **step))


VM = pl.BlockSpec(memory_space=pltpu.VMEM)
SM = pl.BlockSpec(memory_space=pltpu.SMEM)


def project_kernel(nz, wave, *refs):
    pos, own_ref, nb_ref = refs[:3]
    nchunk = 2 * nz
    w_refs = refs[3 : 3 + 2 * nchunk]
    outs = refs[3 + 2 * nchunk : 3 + 2 * nchunk + nz]
    tokp, acc = refs[3 + 2 * nchunk + nz :]
    x, z, y, c = pos[0], pos[1], pos[2], pos[3]
    ntok = own_ref.shape[0]
    piece = w_refs[0].shape[0] // 2
    for s in range(2):
        for k in range(nz):
            for r in range(2):
                row = (lax.rem(z - k + nz, nz) * 2 + (y ^ r)) * 2 + (c ^ s)
                at = pl.multiple_of(row * piece, piece)
                to = ((s * nz + k) * 2 + r) * piece
                tokp[:ntok, to : to + piece] = own_ref[:, pl.ds(at, piece)]
                tokp[ntok:, to : to + piece] = nb_ref[:, pl.ds(at, piece)]
    width = w_refs[0].shape[1]
    for half in range(2):
        for m in range(0, 2 * ntok, 256):
            for n in range(0, width, 256):
                total = None
                for i in range(nchunk):
                    part = jnp.dot(
                        tokp[m : m + 256, i * 2 * piece : (i + 1) * 2 * piece],
                        w_refs[half * nchunk + i][:, n : n + 256],
                        preferred_element_type=jnp.float32,
                    )
                    total = part if total is None else total + part
                acc[x ^ half, m : m + 256, n : n + 256] = total.astype(jnp.bfloat16)
    for k in range(nz):
        head = lax.rem(z + k, nz)
        if wave == "kv":
            at = pl.multiple_of(head * 128, 128)
            outs[k][: 2 * ntok, :128] = acc[0, :, pl.ds(at, 128)]
            outs[k][: 2 * ntok, 128:] = acc[1, :, pl.ds(at, 128)]
            for r in range(2):
                off = pos[4 + r]
                base = pl.multiple_of(off // 16 * 16, 16)
                rows = outs[k][pl.ds(r * ntok + base, 16), :].astype(jnp.float32)
                hit = lax.broadcasted_iota(jnp.int32, rows.shape, 0) == off - base
                row = jnp.sum(jnp.where(hit, rows, 0.0), axis=0, keepdims=True)
                outs[k][2 * ntok + 16 * r : 2 * ntok + 16 * (r + 1), :] = jnp.broadcast_to(
                    row, rows.shape
                ).astype(jnp.bfloat16)
        else:
            hw = nz // 2
            at = pl.multiple_of(lax.rem(head, hw) * 128, 128)
            outs[k][...] = acc[head // hw, :, pl.ds(at, 128)]


def project(nz, wave, pos, own, nb, pieces, hd):
    ntok, depth = own.shape
    rows = 2 * ntok + (32 if wave == "kv" else 0)
    cols = 2 * hd if wave == "kv" else hd
    width = pieces[0].shape[1]
    return pl.pallas_call(
        functools.partial(project_kernel, nz, wave),
        out_shape=[jax.ShapeDtypeStruct((rows, cols), jnp.bfloat16)] * nz,
        in_specs=[SM] + [VM] * (2 + len(pieces)),
        out_specs=[VM] * nz,
        scratch_shapes=[
            pltpu.VMEM((2 * ntok, depth), jnp.bfloat16),
            pltpu.VMEM((2, 2 * ntok, width), jnp.bfloat16),
        ],
        cost_estimate=pl.CostEstimate(
            flops=2 * 2 * ntok * depth * 2 * width,
            bytes_accessed=2 * depth * (2 * ntok + 2 * width),
            transcendentals=0,
        ),
        name="project_" + wave,
    )(pos, own, nb, *pieces)


def attend_kernel(nz, block, nrand, pos, dev_ref, sub_ref, *refs):
    q_refs = refs[:nz]
    kv_refs = refs[nz : 3 * nz]
    outs = refs[3 * nz : 3 * nz + 2 * nz]
    kv, glob = refs[5 * nz :]
    z, y, c = pos[1], pos[2], pos[3]
    hd = q_refs[0].shape[1]
    ntok = outs[0].shape[0]
    nblk = ntok // block
    total = 4 * nz * nblk
    zero = jnp.zeros((block, 2 * hd), jnp.bfloat16)
    kv[:block, :] = zero
    kv[(total + 1) * block :, :] = zero
    glob[...] = jnp.zeros_like(glob)
    for s in range(2):
        for k in range(nz):
            for r in range(2):
                shard = (lax.rem(z - k + nz, nz) * 2 + (y ^ r)) * 2 + (c ^ s)
                at = pl.multiple_of(block + shard * ntok, block)
                ref = kv_refs[s * nz + k]
                kv[pl.ds(at, ntok), :] = ref[r * ntok : (r + 1) * ntok, :]
                row = ref[2 * ntok + 16 * r : 2 * ntok + 16 * (r + 1), :].astype(jnp.float32)
                glob[pl.ds(shard, 1), :] = row[:1, :]
    nglob = 4 * nz
    gk = glob[:, :hd].astype(jnp.bfloat16)
    gv = glob[:, hd:].astype(jnp.bfloat16)
    head = y * nz + z
    nwin, nkey = 3 * block, (3 + nrand) * block
    lane = lax.broadcasted_iota(jnp.int32, (block, nkey + glob.shape[0]), 1)
    scale = hd**-0.5

    def one(q, b):
        where = []
        for j in range(nrand):
            at = (b * 2 * nz + head) * nrand + j
            where.append(pl.multiple_of((dev_ref[at] * nblk + sub_ref[at] + 1) * block, block))
        first = pl.multiple_of(b * block, block)
        keys = jnp.concatenate(
            [kv[pl.ds(first, nwin), :hd]] + [kv[pl.ds(w, block), :hd] for w in where] + [gk], axis=0
        )
        values = jnp.concatenate(
            [kv[pl.ds(first, nwin), hd:]] + [kv[pl.ds(w, block), hd:] for w in where] + [gv], axis=0
        )
        score = lax.dot_general(
            q, keys, (((1,), (1,)), ((), ())), preferred_element_type=jnp.float32
        )
        low = jnp.where(b == 0, block, 0)
        gap = jnp.where(b == total - 1, 2 * block, nwin)
        keep = (lane >= low) & ((lane < gap) | (lane >= nwin)) & (lane < nkey + nglob)
        score = jnp.where(keep, score * scale, -jnp.inf)
        top = jnp.max(score, axis=1, keepdims=True)
        expo = jnp.exp(score - top)
        weights = (expo / jnp.sum(expo, axis=1, keepdims=True)).astype(jnp.bfloat16)
        return jnp.dot(weights, values, preferred_element_type=jnp.float32).astype(jnp.bfloat16)

    for k in range(nz):
        for r in range(2):
            shard = (lax.rem(z - k + nz, nz) * 2 + (y ^ r)) * 2 + c
            out = outs[k * 2 + r]

            def step(j, carry, k=k, r=r, shard=shard, out=out):
                at = pl.multiple_of(j * block, block)
                q = q_refs[k][pl.ds(r * ntok + at, block), :]
                out[pl.ds(at, block), :] = one(q, shard * nblk + j)
                return carry

            lax.fori_loop(0, nblk, step, 0, unroll=True)


def attend(nz, block, pos, dev, sub, qs, kvs, nrand):
    hd = qs[0].shape[1]
    ntok = qs[0].shape[0] // 2
    total = 4 * nz * ntok
    nkey = (3 + nrand) * block
    nglob = 128
    return pl.pallas_call(
        functools.partial(attend_kernel, nz, block, nrand),
        out_shape=[jax.ShapeDtypeStruct((ntok, hd), jnp.bfloat16)] * (2 * nz),
        in_specs=[SM] * 3 + [VM] * (3 * nz),
        out_specs=[VM] * (2 * nz),
        scratch_shapes=[
            pltpu.VMEM((total + 2 * block, 2 * hd), jnp.bfloat16),
            pltpu.VMEM((nglob, 2 * hd), jnp.float32),
        ],
        cost_estimate=pl.CostEstimate(
            flops=4 * 2 * nz * ntok * nkey * hd,
            bytes_accessed=2 * total * 2 * hd,
            transcendentals=2 * nz * ntok * nkey,
        ),
        name="attend",
    )(pos, dev, sub, *qs, *kvs)


def join_kernel(nz, pos, *refs):
    out = refs[-1]
    z, y = pos[1], pos[2]
    hd = refs[0].shape[1]
    for k in range(nz):
        for r in range(2):
            head = (y ^ r) * nz + lax.rem(z + k, nz)
            out[:, pl.ds(pl.multiple_of(head * hd, hd), hd)] = refs[k * 2 + r][...]


def join(nz, pos, parts):
    ntok, hd = parts[0].shape
    return pl.pallas_call(
        functools.partial(join_kernel, nz),
        out_shape=jax.ShapeDtypeStruct((ntok, 2 * nz * hd), jnp.bfloat16),
        in_specs=[SM] + [VM] * (2 * nz),
        out_specs=VM,
        name="join",
    )(pos, *parts)


def gather_weights(nz, mine, theirs, wide):
    other = send(nz, theirs, dy=1)
    near = jnp.concatenate([mine, other], axis=0)
    half = [near] + [send(nz, near, dz=k) for k in range(1, nz)]
    rest = [send(nz, piece, dg=1) for piece in half]
    half_c = [send(nz, piece, dc=1) for piece in half]
    rest_c = [send(nz, piece, dc=1) for piece in rest]
    return half + half_c + rest + rest_c


def local_heads(tokens, w_query, w_keyval, global_off, rand_dev, rand_sub, *, nz, block):
    ntok = tokens.shape[0]
    nhead, nrand = rand_dev.shape[1], rand_dev.shape[2]
    hd = w_query.shape[1] // nhead
    x = lax.axis_index("groups")
    at = lax.axis_index("seq")
    z, y, c = at // 4, at // 2 % 2, at % 2
    off_nb = send(nz, global_off, dy=1)
    pos = jnp.concatenate(
        [jnp.stack([x, z, y, c]).astype(jnp.int32), global_off, off_nb]
    )
    span = nz * hd
    cut = lambda w, start, size: lax.dynamic_slice_in_dim(w, start, size, 1)
    kv_cols = lambda yy: cut(w_keyval, x * 2 * span + yy * span, span)
    q_cols = lambda yy: cut(w_query, yy * span + x * (span // 2), span // 2)
    kv_pieces = gather_weights(nz, kv_cols(y), kv_cols(1 - y), span)
    nb = send(nz, tokens, dy=1)
    q_pieces = gather_weights(nz, q_cols(y), q_cols(1 - y), span // 2)
    kv_out = project(nz, "kv", pos, tokens, nb, kv_pieces, hd)
    kvs = [kv_out[0]] + [send(nz, kv_out[k], dz=k) for k in range(1, nz)]
    kvs = kvs + [send(nz, piece, dc=1) for piece in kvs]
    q_out = project(nz, "q", pos, tokens, nb, q_pieces, hd)
    qs = [q_out[0]] + [send(nz, q_out[k], dz=k) for k in range(1, nz)]
    outs = attend(nz, block, pos, rand_dev.reshape(-1), rand_sub.reshape(-1), qs, kvs, nrand)
    parts = []
    for k in range(nz):
        for r in range(2):
            piece = outs[k * 2 + r]
            parts.append(piece if k == r == 0 else send(nz, piece, dz=-k, dy=r))
    return join(nz, pos, parts)


H = 8
HD = 128
BLOCK = 64
R = 3
BLK_DEV = 4


def padded_2(block, sides, width):
    for axis, dim in sides:
        count = lax.axis_size(axis)
        forward = [(i, i + 1) for i in range(count - 1)]
        backward = [(target, source) for source, target in forward]
        low = lax.ppermute(
            lax.slice_in_dim(block, block.shape[dim] - width, None, axis=dim), axis, forward
        )
        high = lax.ppermute(lax.slice_in_dim(block, 0, width, axis=dim), axis, backward)
        block = jnp.concatenate([low, block, high], axis=dim)
    return block


def fold_rows(left, piece):
    return jnp.dot(left, piece, preferred_element_type=jnp.float32)


def local(tokens, w_query, w_keyval, global_off, rand_dev, rand_sub):
    ntok = tokens.shape[0]
    nseq = lax.axis_size("seq")
    me_index = lax.axis_index("seq")
    nblk = ntok // BLOCK
    inner = H * HD
    glob_rows = lax.all_gather(jnp.take(tokens, global_off, axis=0), "seq", axis=0, tiled=True)
    left_kv = jnp.concatenate([tokens, glob_rows], axis=0)
    query = fold_rows(tokens, lax.all_gather(w_query, "seq", axis=0, tiled=True))
    keyval = fold_rows(left_kv, lax.all_gather(w_keyval, "seq", axis=0, tiled=True))
    query = query.astype(jnp.bfloat16)
    keyval = keyval.astype(jnp.bfloat16)
    glob_kv = keyval[ntok:]
    keyval = keyval[:ntok]
    glob_kv = glob_kv.reshape(glob_kv.shape[0], 2, H, HD)
    padded = padded_2(keyval, (("seq", 0),), BLOCK)
    window = jnp.concatenate(
        [padded[j * BLOCK : j * BLOCK + ntok].reshape(nblk, BLOCK, 2, H, HD) for j in range(3)],
        axis=1,
    )
    capacity = max(2, 3 * BLK_DEV * H * R // (2 * nseq))
    nreq = nblk * H * R
    dev_all = rand_dev.reshape(nseq, nreq)
    sub_all = rand_sub.reshape(nseq, nreq)
    match = (dev_all == me_index).astype(jnp.int32)
    slot_all = jnp.cumsum(match, axis=1) - 1
    head_of = jnp.arange(nreq, dtype=jnp.int32) // R % H
    code_all = head_of[None, :] * nblk + sub_all
    picked = (match[:, None, :] == 1) & (
        slot_all[:, None, :] == jnp.arange(capacity, dtype=jnp.int32)[None, :, None]
    )
    source = jnp.sum(jnp.where(picked, code_all[:, None, :], 0), axis=2)
    tiles = (
        keyval.reshape(nblk, BLOCK, 2, H, HD)
        .transpose(3, 0, 1, 2, 4)
        .reshape(H * nblk, BLOCK, 2 * HD)
    )
    outgoing = jnp.take(tiles, source, axis=0)
    incoming = lax.all_to_all(outgoing, "seq", split_axis=0, concat_axis=0, tiled=True)
    my_dev = lax.dynamic_slice_in_dim(rand_dev, me_index * nblk, nblk, 0).reshape(nreq)
    onehot = (my_dev[:, None] == jnp.arange(nseq, dtype=jnp.int32)[None, :]).astype(jnp.int32)
    my_slot = jnp.sum(onehot * (jnp.cumsum(onehot, axis=0) - 1), axis=1)
    flat_index = my_dev * capacity + my_slot
    fetched = jnp.take(incoming.reshape(nseq * capacity, BLOCK, 2 * HD), flat_index, axis=0)
    fetched = fetched.reshape(nblk, H, R, BLOCK, 2, HD)
    scale = HD ** (-0.5)
    qry = query.reshape(nblk, BLOCK, H, HD)
    s_win = (
        jnp.einsum("bqhd,bkhd->bhqk", qry, window[:, :, 0], preferred_element_type=jnp.float32)
        * scale
    )
    s_rnd = (
        jnp.einsum(
            "bqhd,bhrkd->bhqrk", qry, fetched[:, :, :, :, 0], preferred_element_type=jnp.float32
        ).reshape(nblk, H, BLOCK, R * BLOCK)
        * scale
    )
    s_glb = (
        jnp.einsum("bqhd,ghd->bhqg", qry, glob_kv[:, 0], preferred_element_type=jnp.float32) * scale
    )
    blk_ids = me_index * nblk + jnp.arange(nblk, dtype=jnp.int32)
    left_ok = jnp.repeat((blk_ids > 0)[:, None], BLOCK, axis=1)
    right_ok = jnp.repeat((blk_ids < nseq * nblk - 1)[:, None], BLOCK, axis=1)
    middle_ok = jnp.ones((nblk, BLOCK), dtype=bool)
    window_ok = jnp.concatenate([left_ok, middle_ok, right_ok], axis=1)
    s_win = jnp.where(window_ok[:, None, None, :], s_win, -jnp.inf)
    scores = jnp.concatenate([s_win, s_rnd, s_glb], axis=3)
    highest = jnp.max(scores, axis=3, keepdims=True)
    expo = jnp.exp(scores - highest)
    weights = (expo / jnp.sum(expo, axis=3, keepdims=True)).astype(jnp.bfloat16)
    w_win = weights[..., : 3 * BLOCK]
    w_rnd = weights[..., 3 * BLOCK : 3 * BLOCK + R * BLOCK].reshape(nblk, H, BLOCK, R, BLOCK)
    w_glb = weights[..., 3 * BLOCK + R * BLOCK :]
    ctx = jnp.einsum("bhqk,bkhd->bqhd", w_win, window[:, :, 1], preferred_element_type=jnp.float32)
    ctx = ctx + jnp.einsum(
        "bhqrk,bhrkd->bqhd", w_rnd, fetched[:, :, :, :, 1], preferred_element_type=jnp.float32
    )
    ctx = ctx + jnp.einsum(
        "bhqg,ghd->bqhd", w_glb, glob_kv[:, 1], preferred_element_type=jnp.float32
    )
    return ctx.reshape(ntok, inner).astype(jnp.bfloat16)


def solution(mesh):
    in_specs = (
        P(("groups", "seq"), None),
        P("seq", None),
        P("seq", None),
        P(("groups", "seq")),
        P("groups", None, None),
        P("groups", None, None),
    )
    out_specs = P(("groups", "seq"), None)
    nseq = mesh.shape["seq"]
    body = local
    if mesh.shape["groups"] == 2 and nseq == 2 * H and nseq % 8 == 0:
        body = functools.partial(local_heads, nz=nseq // 4, block=BLOCK)
    return jax.shard_map(body, mesh=mesh, in_specs=in_specs, out_specs=out_specs, check_vma=False)
```
